32 devices in a mesh: expert: 8 (over z, x), pair: 2 (over core), dp: 2 (over y).
Axes of the slice: x: 2, y: 2, z: 4, core: 2. Of those that a mesh axis runs over, the one named last changes fastest.
Arguments:
- tokens: bfloat16 [128, 196, 768], P(('expert', 'pair', 'dp')), may hold values from -96 to 96
- phi: bfloat16 [768, 16], replicated, may hold values from -0.25 to 0.25
- w_in: bfloat16 [8, 768, 3072], P('expert', None, 'pair'), may hold values from -0.21875 to 0.21875
- w_out: bfloat16 [8, 3072, 768], P('expert', 'pair'), may hold values from -0.109375 to 0.109375
- slot_out: bfloat16 [128, 16, 768], P(('expert', 'pair', 'dp')), may hold values from -6 to 6
- grad_out: bfloat16 [128, 196, 768], P(('expert', 'pair', 'dp')), may hold values from -6 to 6
Outputs:
- token_grad: bfloat16 [128, 196, 768], P(('expert', 'pair', 'dp'))
- phi_grad: float32 [768, 16], replicated
- grad_w_in: bfloat16 [8, 768, 3072], P('expert', 'dp', 'pair')
- grad_w_out: bfloat16 [8, 3072, 768], P('expert', 'pair', 'dp')
The draws below stay inside these ranges and needn't reach their ends.
All inputs are finite; a program needn't handle non-finite values.
Results may differ from the reference program's by a relative error of at most 0.0086.
Values may be sent and summed in bfloat16 or wider, within the bound.
A program may use at most 128 MiB of HBM per device.

```python
import jax
import jax.numpy as jnp
from jax import lax

D = 768
FF = 3072
TOKENS_IMG = 196
SLOTS = 2
IMG_DEV = 4
EXPERTS = 8
IMAGES = 128
N_DP = 2


def phi_table(key):
    raw = jax.random.normal(jax.random.fold_in(key, 101), (D, EXPERTS * SLOTS), jnp.float32)
    scaled = jnp.clip(raw, -6.0, 6.0) * D ** (-0.5)
    return jnp.clip(scaled, -0.25, 0.25)


def draw_phi(key, part):
    return phi_table(key).astype(jnp.bfloat16)


def draw_tokens(key, part):
    drawn = jax.random.normal(jax.random.fold_in(key, 202), (IMAGES, TOKENS_IMG, D), jnp.float32)
    return jnp.clip(drawn, -6.0, 6.0).astype(jnp.bfloat16)


def block_levels(own_key, extent, shards, low, top_value):
    gain = 1.0
    for axis_at, blocks in shards:
        draws = jax.random.uniform(jax.random.fold_in(jax.random.fold_in(own_key, 6), axis_at), (blocks,), jnp.float32, low / len(shards), top_value / len(shards))
        gain = gain * jnp.repeat(jnp.exp(draws), extent[axis_at] // blocks).reshape((-1,) + (1,) * (len(extent) - 1 - axis_at))
    return gain


def noise(stream_key, extent, scale, most, cuts=(), held_as=jnp.bfloat16):
    factor_of = block_levels(stream_key, extent, cuts, -0.22, 0.18) if cuts else 1.0
    values = jax.random.normal(stream_key, extent, jnp.float32) * scale * factor_of
    return jnp.minimum(jnp.maximum(values, -most), most).astype(held_as)


def setup_inputs(seed: int = 0) -> dict:
    keys = jax.random.split(jax.random.key(seed), 7)
    tokens = draw_tokens(jax.random.fold_in(keys[6], 71), 0)
    phi = draw_phi(jax.random.fold_in(keys[6], 71), 0)
    w_in = noise(keys[2], (EXPERTS, D, FF), D ** -0.5, 0.21875, ((0, 8), (2, 2)))
    w_out = noise(keys[3], (EXPERTS, FF, D), FF ** -0.5, 0.109375, ((0, 8), (1, 2)))
    slot_out = noise(keys[4], (IMAGES, EXPERTS * SLOTS, D), 1.0, 6.0, ((0, 32),))
    grad_out = noise(keys[5], (IMAGES, TOKENS_IMG, D), 1.0, 6.0, ((0, 32),))
    return {"tokens": tokens, "phi": phi, "w_in": w_in, "w_out": w_out, "slot_out": slot_out, "grad_out": grad_out}


def expert_rows(z_rows, g_rows, w_first, w_second):
    pre = jnp.dot(z_rows, w_first, preferred_element_type=jnp.float32)
    act_full, gelu_back = jax.vjp(jax.nn.gelu, pre)
    act = act_full.astype(jnp.bfloat16)
    dact = lax.dot_general(g_rows, w_second, (((1,), (1,)), ((), ())), preferred_element_type=jnp.float32)
    dpre = gelu_back(dact)[0].astype(jnp.bfloat16)
    grad_second = lax.dot_general(act, g_rows, (((0,), (0,)), ((), ())), preferred_element_type=jnp.float32)
    grad_first = lax.dot_general(z_rows, dpre, (((0,), (0,)), ((), ())), preferred_element_type=jnp.float32)
    back = lax.dot_general(dpre, w_first, (((1,), (1,)), ((), ())), preferred_element_type=jnp.float32)
    return (grad_first, grad_second, back)

def reference(tokens, phi, w_in, w_out, slot_out, grad_out):
    f32 = jnp.float32
    logits = jnp.einsum('bmd,ds->bms', tokens.astype(f32), phi.astype(f32))
    dispatch = jax.nn.softmax(logits, axis=1)
    combine = jax.nn.softmax(logits, axis=2)
    dispatch_low = dispatch.astype(jnp.bfloat16)
    combine_low = combine.astype(jnp.bfloat16)
    slot_in = jnp.einsum('bms,bmd->bsd', dispatch_low.astype(f32), tokens.astype(f32)).astype(jnp.bfloat16)
    slot_grad = jnp.einsum('bms,bmd->bsd', combine_low.astype(f32), grad_out.astype(f32)).astype(jnp.bfloat16)
    groups = IMAGES // (N_DP * IMG_DEV)
    per_expert_in = jnp.transpose(slot_in.reshape(IMAGES, EXPERTS, SLOTS, D), (1, 0, 2, 3))
    per_expert_grad = jnp.transpose(slot_grad.reshape(IMAGES, EXPERTS, SLOTS, D), (1, 0, 2, 3))

    def one_expert(items):
        z_all, g_all, w_first, w_second = items
        z_split = z_all.reshape(groups, N_DP, IMG_DEV, SLOTS, D)
        g_split = g_all.reshape(groups, N_DP, IMG_DEV, SLOTS, D)
        total_first = jnp.zeros((D, FF), f32)
        total_second = jnp.zeros((FF, D), f32)
        backs = []
        for index in range(N_DP):
            z_rows = z_split[:, index].reshape(-1, D)
            g_rows = g_split[:, index].reshape(-1, D)
            grad_first, grad_second, back = expert_rows(z_rows, g_rows, w_first, w_second)
            total_first = total_first + grad_first.astype(jnp.bfloat16).astype(f32)
            total_second = total_second + grad_second.astype(jnp.bfloat16).astype(f32)
            backs.append(back.astype(jnp.bfloat16).reshape(groups, 1, IMG_DEV, SLOTS, D))
        back_all = jnp.concatenate(backs, axis=1).reshape(IMAGES, SLOTS, D)
        return (total_first.astype(jnp.bfloat16), total_second.astype(jnp.bfloat16), back_all)
    grad_w_in, grad_w_out, back_experts = lax.map(one_expert, (per_expert_in, per_expert_grad, w_in, w_out))
    slot_in_grad = jnp.transpose(back_experts, (1, 0, 2, 3)).reshape(IMAGES, EXPERTS * SLOTS, D)
    dispatch_grad = jnp.einsum('bmd,bsd->bms', tokens.astype(f32), slot_in_grad.astype(f32))
    combine_grad = jnp.einsum('bmd,bsd->bms', grad_out.astype(f32), slot_out.astype(f32))
    logit_grad = dispatch * (dispatch_grad - lax.optimization_barrier(jnp.sum(dispatch * dispatch_grad, axis=1, keepdims=True)))
    logit_grad = logit_grad + combine * (combine_grad - lax.optimization_barrier(jnp.sum(combine * combine_grad, axis=2, keepdims=True)))
    logit_low = logit_grad.astype(jnp.bfloat16)
    token_part = jnp.einsum('bms,bsd->bmd', dispatch_low.astype(f32), slot_in_grad.astype(f32))
    token_grad = (token_part + jnp.einsum('bms,ds->bmd', logit_low.astype(f32), phi.astype(f32))).astype(jnp.bfloat16)
    phi_grad = jnp.einsum('bmd,bms->ds', tokens.astype(f32), logit_low.astype(f32))
    return (token_grad, phi_grad, grad_w_in, grad_w_out)
```

```python
import functools
import math

import jax
import jax.numpy as jnp
from jax import lax
from jax.experimental import pallas as pl
from jax.experimental.pallas import tpu as pltpu
from jax.sharding import PartitionSpec as P

MESH = pl.DeviceIdType.MESH
F32 = jnp.float32
BF16 = jnp.bfloat16
NN = (((1,), (0,)), ((), ()))
NT = (((1,), (1,)), ((), ()))
TN = (((0,), (0,)), ((), ()))


def mm(a, b, dims):
    return lax.dot_general(a, b, dims, preferred_element_type=F32)


def chunk_of(size):
    for width in (512, 384, 256, 128):
        if size % width == 0:
            return width
    return size


def kernel(
    n_e, n_p, n_d,
    tok_hbm, phi_ref, win_hbm, wout_hbm, so_hbm, go_hbm,
    tg_hbm, phit_ref, gw1_hbm, gw2_hbm,
    tok, go, so, win, wout, disp, comb, low, sp, stack, zg, recv, act, dpre,
    back, bin_, ret, sigr, phi_acc, ps, pr, qb, fin, tg, gw1, gw2,
    in_sem, w_sem, out_sem,
    a_send, a_recv, y_send, y_recv, c_send, c_recv, c2_send, c2_recv,
    b_send, b_recv, r_send, r_recv, p_send, p_recv, q_send, q_recv, f_send, f_recv, own_sem,
):
    e = lax.axis_index("expert")
    p = lax.axis_index("pair")
    d = lax.axis_index("dp")
    images, toks, width = tok.shape
    slots_all = phit_ref.shape[0]
    rows = zg.shape[2]
    slots = rows // images
    hidden = win.shape[1]
    fc = chunk_of(hidden)
    half = width // n_d

    def dev(ee, pp, dd):
        return {"expert": ee, "pair": pp, "dp": dd}

    def rem(x, n):
        return lax.rem(x, n)

    def rcopy(src, dst, ss, rs, where):
        return pltpu.make_async_remote_copy(
            src_ref=src, dst_ref=dst, send_sem=ss, recv_sem=rs, device_id=where, device_id_type=MESH
        )

    e_at = [rem(e + k, n_e) for k in range(n_e)]
    e_from = [rem(e + n_e - k, n_e) for k in range(n_e)]
    p_at = [rem(p + k, n_p) for k in range(n_p)]
    p_from = [rem(p + n_p - k, n_p) for k in range(n_p)]
    d_at = [rem(d + k, n_d) for k in range(n_d)]
    d_from = [rem(d + n_d - k, n_d) for k in range(n_d)]

    barrier = pltpu.get_barrier_semaphore()
    peers = [dev(e_at[k], p, d) for k in range(1, n_e)]
    peers += [dev(e, p_at[i], d_at[j]) for i in range(n_p) for j in range(n_d) if i or j]
    for peer in peers:
        pl.semaphore_signal(barrier, inc=1, device_id=peer, device_id_type=MESH)

    loads = []
    for b in range(images):
        pair = (
            pltpu.make_async_copy(tok_hbm.at[b], tok.at[b], in_sem.at[2 * b]),
            pltpu.make_async_copy(go_hbm.at[b], go.at[b], in_sem.at[2 * b + 1]),
        )
        pair[0].start()
        pair[1].start()
        loads.append(pair)
    w_loads = [
        pltpu.make_async_copy(win_hbm.at[0], win, w_sem.at[0]),
        pltpu.make_async_copy(wout_hbm.at[0], wout, w_sem.at[1]),
        pltpu.make_async_copy(so_hbm, so, w_sem.at[2]),
    ]
    for w_load in w_loads:
        w_load.start()

    phi_t = phi_ref[...].astype(F32).T.astype(BF16)
    total = images * slots_all
    r_at = lax.broadcasted_iota(jnp.int32, (total, total), 0)
    c_at = lax.broadcasted_iota(jnp.int32, (total, total), 1)
    src_of = ((r_at % rows) // slots) * slots_all + (r_at // rows) * slots + r_at % slots
    perm = jnp.where(src_of == c_at, 1.0, 0.0).astype(BF16)

    for b in range(images):
        loads[b][0].wait()
        logits = mm(phi_t, tok[b], NT)
        by_tok = jnp.exp(logits - jnp.max(logits, axis=1, keepdims=True))
        by_tok = by_tok / jnp.sum(by_tok, axis=1, keepdims=True)
        by_slot = jnp.exp(logits - jnp.max(logits, axis=0, keepdims=True))
        by_slot = by_slot / jnp.sum(by_slot, axis=0, keepdims=True)
        disp[b] = by_tok
        comb[b] = by_slot
        low[b, pl.ds(0, slots_all), :] = by_tok.astype(BF16)
        stack[0, pl.ds(b * slots_all, slots_all), :] = mm(by_tok.astype(BF16), tok[b], NN).astype(BF16)
        loads[b][1].wait()
        stack[1, pl.ds(b * slots_all, slots_all), :] = mm(by_slot.astype(BF16), go[b], NN).astype(BF16)
    for which in range(2):
        moved = mm(perm, stack[which], NN).astype(BF16)
        zg[which] = moved.reshape(n_e, rows, width)

    pl.semaphore_wait(barrier, len(peers))

    out_a = []
    for k in range(1, n_e):
        cp = rcopy(
            zg.at[:, e_at[k]], recv.at[:, d, p, e], a_send.at[k], a_recv.at[k], dev(e_at[k], p, d)
        )
        cp.start()
        out_a.append(cp)
    own = pltpu.make_async_copy(zg.at[:, e], recv.at[:, d, p, e], own_sem.at[0])
    own.start()

    w_loads[2].wait()
    for b in range(images):
        cg = mm(so[b], go[b], NT)
        cm = comb[b]
        comb[b] = cm * (cg - jnp.sum(cm * cg, axis=0, keepdims=True))

    out_y, out_c, out_c2 = [], [], []
    for k in range(n_e):
        blk = recv.at[:, d, p, e_from[k]]
        if k == 0:
            own.wait()
        else:
            rcopy(blk, blk, a_send.at[k], a_recv.at[k], dev(e, p, d)).wait_recv()
        for i in range(1, n_p):
            cp = rcopy(blk, blk, c_send.at[i, k], c_recv.at[i, k], dev(e, p_at[i], d))
            cp.start()
            out_c.append(cp)
        for j in range(1, n_d):
            cp = rcopy(blk, blk, y_send.at[j, k], y_recv.at[j, k], dev(e, p, d_at[j]))
            cp.start()
            out_y.append(cp)
    for cp in w_loads[:2]:
        cp.wait()
    for i in range(1, n_p):
        for k in range(n_e):
            blk = recv.at[:, d, p_from[i], e_from[k]]
            rcopy(blk, blk, c_send.at[i, k], c_recv.at[i, k], dev(e, p, d)).wait_recv()

    group_rows = n_p * n_e * rows
    part_rows = n_e * rows
    c1 = math.sqrt(2.0 / math.pi)

    def hidden_pass(group, with_back):
        z = recv[0, group].reshape(group_rows, width)
        g = recv[1, group].reshape(group_rows, width)

        def step(c, carry):
            cols = pl.ds(pl.multiple_of(c * fc, fc), fc)
            x = mm(z, win[:, cols], NN)
            da = mm(g, wout[cols, :], NT)
            x2 = x * x
            th = jnp.tanh(c1 * (x + 0.044715 * (x2 * x)))
            cdf = 0.5 * (1.0 + th)
            slope = cdf + (0.5 * c1) * x * (1.0 - th * th) * (1.0 + (3.0 * 0.044715) * x2)
            act[group, :, cols] = (x * cdf).astype(BF16)
            dp_low = (da * slope).astype(BF16)
            dpre[group, :, cols] = dp_low
            if with_back:
                term = mm(dp_low, win[:, cols], NT).reshape(n_p, part_rows, width)

                @pl.when(c == 0)
                def _():
                    back[...] = term

                @pl.when(c > 0)
                def _():
                    back[...] = back[...] + term

            return carry

        lax.fori_loop(0, hidden // fc, step, 0)

    hidden_pass(d, True)

    out_b = []
    for i in range(1, n_p):
        cp = rcopy(back.at[p_at[i]], bin_.at[i - 1], b_send.at[i], b_recv.at[i], dev(e, p_at[i], d))
        cp.start()
        out_b.append(cp)

    for j in range(1, n_d):
        for k in range(n_e):
            blk = recv.at[:, d_from[j], p, e_from[k]]
            rcopy(blk, blk, y_send.at[j, k], y_recv.at[j, k], dev(e, p, d)).wait_recv()
            for i in range(1, n_p):
                cp = rcopy(blk, blk, c2_send.at[j, i, k], c2_recv.at[j, i, k], dev(e, p_at[i], d))
                cp.start()
                out_c2.append(cp)

    acc = back[p]
    for i in range(1, n_p):
        rcopy(bin_.at[i - 1], bin_.at[i - 1], b_send.at[i], b_recv.at[i], dev(e, p, d)).wait_recv()
        acc = acc + bin_[i - 1]
    ret[...] = acc.astype(BF16).reshape(n_e, rows, width)
    out_r = []
    for k in range(1, n_e):
        cp = rcopy(ret.at[e_at[k]], sigr.at[e], r_send.at[k], r_recv.at[k], dev(e_at[k], p, d))
        cp.start()
        out_r.append(cp)
    sigr[e] = ret[e]

    for j in range(1, n_d):
        for i in range(1, n_p):
            for k in range(n_e):
                blk = recv.at[:, d_from[j], p_from[i], e_from[k]]
                rcopy(blk, blk, c2_send.at[j, i, k], c2_recv.at[j, i, k], dev(e, p, d)).wait_recv()
        hidden_pass(d_from[j], False)

    my_half = pl.ds(pl.multiple_of(d * half, half), half)

    def grads_in(c, carry):
        cols = pl.ds(pl.multiple_of(c * fc, fc), fc)
        s1 = None
        for gi in range(n_d):
            z = recv[0, gi, :, :, :, my_half].reshape(group_rows, half)
            g1 = mm(z, dpre[gi, :, cols], TN).astype(BF16).astype(F32)
            s1 = g1 if s1 is None else s1 + g1
        gw1[:, cols] = s1.astype(BF16)
        return carry

    def grads_out(c, carry):
        cols = pl.ds(pl.multiple_of(c * fc, fc), fc)
        s2 = None
        for gi in range(n_d):
            g = recv[1, gi, :, :, :, my_half].reshape(group_rows, half)
            g2 = mm(act[gi, :, cols], g, TN).astype(BF16).astype(F32)
            s2 = g2 if s2 is None else s2 + g2
        gw2[cols, :] = s2.astype(BF16)
        return carry

    lax.fori_loop(0, hidden // fc, grads_in, 0)
    outs = [pltpu.make_async_copy(gw1, gw1_hbm.at[0], out_sem.at[0])]
    outs[0].start()

    for k in range(1, n_e):
        blk = sigr.at[e_from[k]]
        rcopy(blk, blk, r_send.at[k], r_recv.at[k], dev(e, p, d)).wait_recv()

    sig_all = mm(perm, sigr[...].reshape(total, width), TN).astype(BF16)
    phi_sum = None
    for b in range(images):
        sig = sig_all[b * slots_all:(b + 1) * slots_all]
        sp[b, pl.ds(0, slots_all), :] = sig
        sp[b, pl.ds(slots_all, slots_all), :] = phi_t
        dg = mm(sig, tok[b], NT)
        dm = disp[b]
        lg = dm * (dg - jnp.sum(dm * dg, axis=1, keepdims=True)) + comb[b]
        lg_low = lg.astype(BF16)
        low[b, pl.ds(slots_all, slots_all), :] = lg_low
        term = mm(lg_low, tok[b], NN)
        phi_sum = term if phi_sum is None else phi_sum + term
    phi_acc[...] = phi_sum
    for k in range(n_e):
        ps[k] = phi_acc[pl.ds(k * slots, slots), :]
    out_p = []
    for k in range(1, n_e):
        cp = rcopy(ps.at[e_at[k]], pr.at[e], p_send.at[k], p_recv.at[k], dev(e_at[k], p, d))
        cp.start()
        out_p.append(cp)
    pr[e] = ps[e]

    for b in range(images):
        tg[b] = mm(low[b], sp[b], TN).astype(BF16)
        cp = pltpu.make_async_copy(tg.at[b], tg_hbm.at[b], out_sem.at[2 + b])
        cp.start()
        outs.append(cp)

    for k in range(1, n_e):
        blk = pr.at[e_from[k]]
        rcopy(blk, blk, p_send.at[k], p_recv.at[k], dev(e, p, d)).wait_recv()
    qb[d, p] = jnp.sum(pr[...], axis=0)
    out_q = []
    for j in range(n_d):
        for i in range(n_p):
            if i or j:
                cp = rcopy(
                    qb.at[d, p], qb.at[d, p], q_send.at[j, i], q_recv.at[j, i], dev(e, p_at[i], d_at[j])
                )
                cp.start()
                out_q.append(cp)

    lax.fori_loop(0, hidden // fc, grads_out, 0)
    cp = pltpu.make_async_copy(gw2, gw2_hbm.at[0], out_sem.at[1])
    cp.start()
    outs.append(cp)

    for j in range(n_d):
        for i in range(n_p):
            if i or j:
                blk = qb.at[d_from[j], p_from[i]]
                rcopy(blk, blk, q_send.at[j, i], q_recv.at[j, i], dev(e, p, d)).wait_recv()
    whole = None
    for j in range(n_d):
        for i in range(n_p):
            whole = qb[j, i] if whole is None else whole + qb[j, i]
    fin[e] = whole
    out_f = []
    for k in range(1, n_e):
        cp = rcopy(fin.at[e], fin.at[e], f_send.at[k], f_recv.at[k], dev(e_at[k], p, d))
        cp.start()
        out_f.append(cp)
    for group in (out_a, out_y, out_c, out_c2, out_b, out_r, out_p, out_q):
        for cp in group:
            cp.wait_send()
    for cp in outs:
        cp.wait()
    for k in range(1, n_e):
        blk = fin.at[e_from[k]]
        rcopy(blk, blk, f_send.at[k], f_recv.at[k], dev(e, p, d)).wait_recv()
    for k in range(n_e):
        phit_ref[pl.ds(k * slots, slots), :] = fin[k]
    for cp in out_f:
        cp.wait_send()


def local(n_e, n_p, n_d, tokens, phi, w_in, w_out, slot_out, grad_out):
    images, toks, width = tokens.shape
    slots_all = phi.shape[1]
    hidden = w_in.shape[2]
    slots = slots_all // n_e
    rows = images * slots
    half = width // n_d
    group = n_p * n_e * rows
    vm = pltpu.VMEM
    sem = pltpu.SemaphoreType.DMA
    scratch = [
        vm((images, toks, width), BF16),
        vm((images, toks, width), BF16),
        vm((images, slots_all, width), BF16),
        vm((width, hidden), BF16),
        vm((hidden, width), BF16),
        vm((images, slots_all, toks), F32),
        vm((images, slots_all, toks), F32),
        vm((images, 2 * slots_all, toks), BF16),
        vm((images, 2 * slots_all, width), BF16),
        vm((2, images * slots_all, width), BF16),
        vm((2, n_e, rows, width), BF16),
        vm((2, n_d, n_p, n_e, rows, width), BF16),
        vm((n_d, group, hidden), BF16),
        vm((n_d, group, hidden), BF16),
        vm((n_p, n_e * rows, width), F32),
        vm((n_p - 1, n_e * rows, width), F32),
        vm((n_e, rows, width), BF16),
        vm((n_e, rows, width), BF16),
        vm((slots_all, width), F32),
        vm((n_e, slots, width), F32),
        vm((n_e, slots, width), F32),
        vm((n_d, n_p, slots, width), F32),
        vm((n_e, slots, width), F32),
        vm((images, toks, width), BF16),
        vm((half, hidden), BF16),
        vm((hidden, half), BF16),
        sem((2 * images,)),
        sem((3,)),
        sem((2 + images,)),
    ]
    scratch += [sem((n_e,))] * 2
    scratch += [sem((n_d, n_e))] * 2
    scratch += [sem((n_p, n_e))] * 2
    scratch += [sem((n_d, n_p, n_e))] * 2
    scratch += [sem((n_p,))] * 2
    scratch += [sem((n_e,))] * 2
    scratch += [sem((n_e,))] * 2
    scratch += [sem((n_d, n_p))] * 2
    scratch += [sem((n_e,))] * 2
    scratch += [sem((1,))]
    hbm = pl.BlockSpec(memory_space=pl.ANY)
    vmem = pl.BlockSpec(memory_space=pltpu.VMEM)
    token_grad, phi_t, gw1, gw2 = pl.pallas_call(
        functools.partial(kernel, n_e, n_p, n_d),
        out_shape=(
            jax.ShapeDtypeStruct((images, toks, width), BF16),
            jax.ShapeDtypeStruct((slots_all, width), F32),
            jax.ShapeDtypeStruct((1, half, hidden), BF16),
            jax.ShapeDtypeStruct((1, hidden, half), BF16),
        ),
        in_specs=[hbm, vmem, hbm, hbm, hbm, hbm],
        out_specs=(hbm, vmem, hbm, hbm),
        scratch_shapes=scratch,
        compiler_params=pltpu.CompilerParams(collective_id=0, has_side_effects=True),
    )(tokens, phi, w_in, w_out, slot_out, grad_out)
    return (token_grad, phi_t.T, gw1, gw2)


def solution(mesh):
    in_specs = (
        P(("expert", "pair", "dp"), None, None),
        P(),
        P("expert", None, "pair"),
        P("expert", "pair", None),
        P(("expert", "pair", "dp"), None, None),
        P(("expert", "pair", "dp"), None, None),
    )
    out_specs = (
        P(("expert", "pair", "dp"), None, None),
        P(),
        P("expert", "dp", "pair"),
        P("expert", "pair", "dp"),
    )
    body = functools.partial(local, mesh.shape["expert"], mesh.shape["pair"], mesh.shape["dp"])
    return jax.shard_map(body, mesh=mesh, in_specs=in_specs, out_specs=out_specs, check_vma=False)
```

```python
import functools
import math

import jax
import jax.numpy as jnp
from jax import lax
from jax.experimental import pallas as pl
from jax.experimental.pallas import tpu as pltpu
from jax.sharding import PartitionSpec as P

MESH = pl.DeviceIdType.MESH
F32 = jnp.float32
BF16 = jnp.bfloat16
NN = (((1,), (0,)), ((), ()))
NT = (((1,), (1,)), ((), ()))
TN = (((0,), (0,)), ((), ()))


def mm(a, b, dims):
    return lax.dot_general(a, b, dims, preferred_element_type=F32)


def chunk_of(size):
    for width in (512, 384, 256, 128):
        if size % width == 0:
            return width
    return size


def kernel(
    n_e, n_p, n_d,
    tok_hbm, phi_ref, win_hbm, wout_hbm, so_hbm, go_hbm,
    tg_hbm, phit_ref, gw1_hbm, gw2_hbm,
    tok3, go3, tok, go, so, win, wout, disp, comb, low, sp, zg, recv, act, dpre,
    back, bin_, ret, sigr, phi_acc, ps, pr, qb, fin, tg, gw1, gw2,
    in_sem, w_sem, out_sem,
    a_send, a_recv, y_send, y_recv, c_send, c_recv, c2_send, c2_recv,
    b_send, b_recv, r_send, r_recv, p_send, p_recv, q_send, q_recv, f_send, f_recv, own_sem,
):
    e = lax.axis_index("expert")
    p = lax.axis_index("pair")
    d = lax.axis_index("dp")
    toks, images, width = tok3.shape
    slots_all = phit_ref.shape[0]
    rows = zg.shape[2]
    slots = rows // images
    hidden = win.shape[1]
    fc = chunk_of(hidden)
    half = width // n_d

    def dev(ee, pp, dd):
        return {"expert": ee, "pair": pp, "dp": dd}

    def rem(x, n):
        return lax.rem(x, n)

    def rcopy(src, dst, ss, rs, where):
        return pltpu.make_async_remote_copy(
            src_ref=src, dst_ref=dst, send_sem=ss, recv_sem=rs, device_id=where, device_id_type=MESH
        )

    e_at = [rem(e + k, n_e) for k in range(n_e)]
    e_from = [rem(e + n_e - k, n_e) for k in range(n_e)]
    p_at = [rem(p + k, n_p) for k in range(n_p)]
    p_from = [rem(p + n_p - k, n_p) for k in range(n_p)]
    d_at = [rem(d + k, n_d) for k in range(n_d)]
    d_from = [rem(d + n_d - k, n_d) for k in range(n_d)]

    barrier = pltpu.get_barrier_semaphore()
    peers = [dev(e_at[k], p, d) for k in range(1, n_e)]
    peers += [dev(e, p_at[i], d_at[j]) for i in range(n_p) for j in range(n_d) if i or j]
    for peer in peers:
        pl.semaphore_signal(barrier, inc=1, device_id=peer, device_id_type=MESH)

    loads = [
        pltpu.make_async_copy(tok_hbm, tok3, in_sem.at[0]),
        pltpu.make_async_copy(go_hbm, go3, in_sem.at[1]),
    ]
    for load in loads:
        load.start()
    w_loads = [
        pltpu.make_async_copy(win_hbm.at[0], win, w_sem.at[0]),
        pltpu.make_async_copy(wout_hbm.at[0], wout, w_sem.at[1]),
        pltpu.make_async_copy(so_hbm, so, w_sem.at[2]),
    ]
    for w_load in w_loads:
        w_load.start()

    total = images * slots_all
    lanes = toks * images

    def pick(columns, index_of):
        r_at = lax.broadcasted_iota(jnp.int32, (total, columns), 0)
        c_at = lax.broadcasted_iota(jnp.int32, (total, columns), 1)
        return jnp.where(index_of(r_at) == c_at, 1.0, 0.0).astype(BF16)

    def slot_of(r):
        return (r // rows) * slots + r % slots

    def image_of(r):
        return (r % rows) // slots

    phi_x = mm(pick(slots_all, slot_of), phi_ref[...], NN).astype(BF16)
    sp[pl.ds(total, total), :] = phi_x
    r_at = lax.broadcasted_iota(jnp.int32, (total, lanes), 0)
    l_at = lax.broadcasted_iota(jnp.int32, (total, lanes), 1)
    same = image_of(r_at) == l_at % images

    loads[0].wait()
    tok[...] = tok3[...].reshape(lanes, width)
    logits = jnp.where(same, mm(phi_x, tok[...], NT), -jnp.inf)
    by_tok = jnp.exp(logits - jnp.max(logits, axis=1, keepdims=True))
    by_tok = by_tok / jnp.sum(by_tok, axis=1, keepdims=True)
    disp[...] = by_tok
    low[pl.ds(0, total), :] = by_tok.astype(BF16)
    zg[0] = mm(by_tok.astype(BF16), tok[...], NN).astype(BF16).reshape(n_e, rows, width)
    by_slot = jnp.exp(logits - jnp.max(logits, axis=0, keepdims=True))
    by_slot = by_slot / jnp.sum(by_slot, axis=0, keepdims=True)
    comb[...] = by_slot
    loads[1].wait()
    go[...] = go3[...].reshape(lanes, width)
    zg[1] = mm(by_slot.astype(BF16), go[...], NN).astype(BF16).reshape(n_e, rows, width)

    pl.semaphore_wait(barrier, len(peers))

    out_a = []
    for k in range(1, n_e):
        cp = rcopy(
            zg.at[:, e_at[k]], recv.at[:, d, p, e], a_send.at[k], a_recv.at[k], dev(e_at[k], p, d)
        )
        cp.start()
        out_a.append(cp)
    own = pltpu.make_async_copy(zg.at[:, e], recv.at[:, d, p, e], own_sem.at[0])
    own.start()

    w_loads[2].wait()
    so_x = mm(
        pick(total, lambda r: image_of(r) * slots_all + slot_of(r)), so[...].reshape(total, width), NN
    ).astype(BF16)
    cm = comb[...]
    cg = mm(so_x, go[...], NT)
    comb[...] = cm * (cg - jnp.sum(cm * cg, axis=0, keepdims=True))

    out_y, out_c, out_c2 = [], [], []
    for k in range(n_e):
        blk = recv.at[:, d, p, e_from[k]]
        if k == 0:
            own.wait()
        else:
            rcopy(blk, blk, a_send.at[k], a_recv.at[k], dev(e, p, d)).wait_recv()
        for i in range(1, n_p):
            cp = rcopy(blk, blk, c_send.at[i, k], c_recv.at[i, k], dev(e, p_at[i], d))
            cp.start()
            out_c.append(cp)
        for j in range(1, n_d):
            cp = rcopy(blk, blk, y_send.at[j, k], y_recv.at[j, k], dev(e, p, d_at[j]))
            cp.start()
            out_y.append(cp)
    for cp in w_loads[:2]:
        cp.wait()
    for i in range(1, n_p):
        for k in range(n_e):
            blk = recv.at[:, d, p_from[i], e_from[k]]
            rcopy(blk, blk, c_send.at[i, k], c_recv.at[i, k], dev(e, p, d)).wait_recv()

    group_rows = n_p * n_e * rows
    part_rows = n_e * rows
    c1 = math.sqrt(2.0 / math.pi)

    def hidden_pass(group, with_back):
        z = recv[0, group].reshape(group_rows, width)
        g = recv[1, group].reshape(group_rows, width)

        def step(c, carry):
            cols = pl.ds(pl.multiple_of(c * fc, fc), fc)
            x = mm(z, win[:, cols], NN)
            da = mm(g, wout[cols, :], NT)
            x2 = x * x
            th = jnp.tanh(c1 * (x + 0.044715 * (x2 * x)))
            cdf = 0.5 * (1.0 + th)
            slope = cdf + (0.5 * c1) * x * (1.0 - th * th) * (1.0 + (3.0 * 0.044715) * x2)
            act[group, :, cols] = (x * cdf).astype(BF16)
            dp_low = (da * slope).astype(BF16)
            dpre[group, :, cols] = dp_low
            if with_back:
                term = mm(dp_low, win[:, cols], NT).reshape(n_p, part_rows, width)

                @pl.when(c == 0)
                def _():
                    back[...] = term

                @pl.when(c > 0)
                def _():
                    back[...] = back[...] + term

            return carry

        lax.fori_loop(0, hidden // fc, step, 0)

    hidden_pass(d, True)

    out_b = []
    for i in range(1, n_p):
        cp = rcopy(back.at[p_at[i]], bin_.at[i - 1], b_send.at[i], b_recv.at[i], dev(e, p_at[i], d))
        cp.start()
        out_b.append(cp)

    for j in range(1, n_d):
        for k in range(n_e):
            blk = recv.at[:, d_from[j], p, e_from[k]]
            rcopy(blk, blk, y_send.at[j, k], y_recv.at[j, k], dev(e, p, d)).wait_recv()
            for i in range(1, n_p):
                cp = rcopy(blk, blk, c2_send.at[j, i, k], c2_recv.at[j, i, k], dev(e, p_at[i], d))
                cp.start()
                out_c2.append(cp)

    acc = back[p]
    for i in range(1, n_p):
        rcopy(bin_.at[i - 1], bin_.at[i - 1], b_send.at[i], b_recv.at[i], dev(e, p, d)).wait_recv()
        acc = acc + bin_[i - 1]
    ret[...] = acc.astype(BF16).reshape(n_e, rows, width)
    out_r = []
    for k in range(1, n_e):
        cp = rcopy(ret.at[e_at[k]], sigr.at[e], r_send.at[k], r_recv.at[k], dev(e_at[k], p, d))
        cp.start()
        out_r.append(cp)
    sigr[e] = ret[e]

    for j in range(1, n_d):
        for i in range(1, n_p):
            for k in range(n_e):
                blk = recv.at[:, d_from[j], p_from[i], e_from[k]]
                rcopy(blk, blk, c2_send.at[j, i, k], c2_recv.at[j, i, k], dev(e, p, d)).wait_recv()
        hidden_pass(d_from[j], False)

    my_half = pl.ds(pl.multiple_of(d * half, half), half)

    def grads_in(c, carry):
        cols = pl.ds(pl.multiple_of(c * fc, fc), fc)
        s1 = None
        for gi in range(n_d):
            z = recv[0, gi, :, :, :, my_half].reshape(group_rows, half)
            g1 = mm(z, dpre[gi, :, cols], TN).astype(BF16).astype(F32)
            s1 = g1 if s1 is None else s1 + g1
        gw1[:, cols] = s1.astype(BF16)
        return carry

    def grads_out(c, carry):
        cols = pl.ds(pl.multiple_of(c * fc, fc), fc)
        s2 = None
        for gi in range(n_d):
            g = recv[1, gi, :, :, :, my_half].reshape(group_rows, half)
            g2 = mm(act[gi, :, cols], g, TN).astype(BF16).astype(F32)
            s2 = g2 if s2 is None else s2 + g2
        gw2[cols, :] = s2.astype(BF16)
        return carry

    lax.fori_loop(0, hidden // fc, grads_in, 0)
    outs = [pltpu.make_async_copy(gw1, gw1_hbm.at[0], out_sem.at[0])]
    outs[0].start()

    for k in range(1, n_e):
        blk = sigr.at[e_from[k]]
        rcopy(blk, blk, r_send.at[k], r_recv.at[k], dev(e, p, d)).wait_recv()

    sig = sigr[...].reshape(total, width)
    dg = mm(sig, tok[...], NT)
    dm = disp[...]
    lg_low = (dm * (dg - jnp.sum(dm * dg, axis=1, keepdims=True)) + comb[...]).astype(BF16)
    phi_acc[...] = mm(lg_low, tok[...], NN)
    for k in range(n_e):
        piece = None
        for b in range(images):
            term = phi_acc[pl.ds(k * rows + b * slots, slots), :]
            piece = term if piece is None else piece + term
        ps[k] = piece
    out_p = []
    for k in range(1, n_e):
        cp = rcopy(ps.at[e_at[k]], pr.at[e], p_send.at[k], p_recv.at[k], dev(e_at[k], p, d))
        cp.start()
        out_p.append(cp)
    pr[e] = ps[e]

    low[pl.ds(total, total), :] = lg_low
    sp[pl.ds(0, total), :] = sig
    tg[...] = mm(low[...], sp[...], TN).astype(BF16).reshape(toks, images, width)
    cp = pltpu.make_async_copy(tg, tg_hbm, out_sem.at[2])
    cp.start()
    outs.append(cp)

    for k in range(1, n_e):
        blk = pr.at[e_from[k]]
        rcopy(blk, blk, p_send.at[k], p_recv.at[k], dev(e, p, d)).wait_recv()
    qb[d, p] = jnp.sum(pr[...], axis=0)
    out_q = []
    for j in range(n_d):
        for i in range(n_p):
            if i or j:
                cp = rcopy(
                    qb.at[d, p], qb.at[d, p], q_send.at[j, i], q_recv.at[j, i], dev(e, p_at[i], d_at[j])
                )
                cp.start()
                out_q.append(cp)

    lax.fori_loop(0, hidden // fc, grads_out, 0)
    cp = pltpu.make_async_copy(gw2, gw2_hbm.at[0], out_sem.at[1])
    cp.start()
    outs.append(cp)

    for j in range(n_d):
        for i in range(n_p):
            if i or j:
                blk = qb.at[d_from[j], p_from[i]]
                rcopy(blk, blk, q_send.at[j, i], q_recv.at[j, i], dev(e, p, d)).wait_recv()
    whole = None
    for j in range(n_d):
        for i in range(n_p):
            whole = qb[j, i] if whole is None else whole + qb[j, i]
    fin[e] = whole
    out_f = []
    for k in range(1, n_e):
        cp = rcopy(fin.at[e], fin.at[e], f_send.at[k], f_recv.at[k], dev(e_at[k], p, d))
        cp.start()
        out_f.append(cp)
    for group in (out_a, out_y, out_c, out_c2, out_b, out_r, out_p, out_q):
        for cp in group:
            cp.wait_send()
    for cp in outs:
        cp.wait()
    for k in range(1, n_e):
        blk = fin.at[e_from[k]]
        rcopy(blk, blk, f_send.at[k], f_recv.at[k], dev(e, p, d)).wait_recv()
    for k in range(n_e):
        phit_ref[pl.ds(k * slots, slots), :] = fin[k]
    for cp in out_f:
        cp.wait_send()


def local(n_e, n_p, n_d, tokens, phi, w_in, w_out, slot_out, grad_out):
    images, toks, width = tokens.shape
    slots_all = phi.shape[1]
    hidden = w_in.shape[2]
    slots = slots_all // n_e
    rows = images * slots
    half = width // n_d
    group = n_p * n_e * rows
    vm = pltpu.VMEM
    sem = pltpu.SemaphoreType.DMA
    scratch = [
        vm((toks, images, width), BF16),
        vm((toks, images, width), BF16),
        vm((toks * images, width), BF16),
        vm((toks * images, width), BF16),
        vm((images, slots_all, width), BF16),
        vm((width, hidden), BF16),
        vm((hidden, width), BF16),
        vm((images * slots_all, toks * images), F32),
        vm((images * slots_all, toks * images), F32),
        vm((2 * images * slots_all, toks * images), BF16),
        vm((2 * images * slots_all, width), BF16),
        vm((2, n_e, rows, width), BF16),
        vm((2, n_d, n_p, n_e, rows, width), BF16),
        vm((n_d, group, hidden), BF16),
        vm((n_d, group, hidden), BF16),
        vm((n_p, n_e * rows, width), F32),
        vm((n_p - 1, n_e * rows, width), F32),
        vm((n_e, rows, width), BF16),
        vm((n_e, rows, width), BF16),
        vm((images * slots_all, width), F32),
        vm((n_e, slots, width), F32),
        vm((n_e, slots, width), F32),
        vm((n_d, n_p, slots, width), F32),
        vm((n_e, slots, width), F32),
        vm((toks, images, width), BF16),
        vm((half, hidden), BF16),
        vm((hidden, half), BF16),
        sem((2,)),
        sem((3,)),
        sem((3,)),
    ]
    scratch += [sem((n_e,))] * 2
    scratch += [sem((n_d, n_e))] * 2
    scratch += [sem((n_p, n_e))] * 2
    scratch += [sem((n_d, n_p, n_e))] * 2
    scratch += [sem((n_p,))] * 2
    scratch += [sem((n_e,))] * 2
    scratch += [sem((n_e,))] * 2
    scratch += [sem((n_d, n_p))] * 2
    scratch += [sem((n_e,))] * 2
    scratch += [sem((1,))]
    hbm = pl.BlockSpec(memory_space=pl.ANY)
    vmem = pl.BlockSpec(memory_space=pltpu.VMEM)
    token_grad, phi_t, gw1, gw2 = pl.pallas_call(
        functools.partial(kernel, n_e, n_p, n_d),
        out_shape=(
            jax.ShapeDtypeStruct((toks, images, width), BF16),
            jax.ShapeDtypeStruct((slots_all, width), F32),
            jax.ShapeDtypeStruct((1, half, hidden), BF16),
            jax.ShapeDtypeStruct((1, hidden, half), BF16),
        ),
        in_specs=[hbm, vmem, hbm, hbm, hbm, hbm],
        out_specs=(hbm, vmem, hbm, hbm),
        scratch_shapes=scratch,
        compiler_params=pltpu.CompilerParams(collective_id=0, has_side_effects=True),
    )(
        jnp.transpose(tokens, (1, 0, 2)), phi.T, w_in, w_out, slot_out, jnp.transpose(grad_out, (1, 0, 2))
    )
    return (jnp.transpose(token_grad, (1, 0, 2)), phi_t.T, gw1, gw2)


def solution(mesh):
    in_specs = (
        P(("expert", "pair", "dp"), None, None),
        P(),
        P("expert", None, "pair"),
        P("expert", "pair", None),
        P(("expert", "pair", "dp"), None, None),
        P(("expert", "pair", "dp"), None, None),
    )
    out_specs = (
        P(("expert", "pair", "dp"), None, None),
        P(),
        P("expert", "dp", "pair"),
        P("expert", "pair", "dp"),
    )
    body = functools.partial(local, mesh.shape["expert"], mesh.shape["pair"], mesh.shape["dp"])
    return jax.shard_map(body, mesh=mesh, in_specs=in_specs, out_specs=out_specs, check_vma=False)
```

```python
import functools
import math

import jax
import jax.numpy as jnp
from jax import lax
from jax.experimental import pallas as pl
from jax.experimental.pallas import tpu as pltpu
from jax.sharding import PartitionSpec as P

MESH = pl.DeviceIdType.MESH
F32 = jnp.float32
BF16 = jnp.bfloat16
NN = (((1,), (0,)), ((), ()))
NT = (((1,), (1,)), ((), ()))
TN = (((0,), (0,)), ((), ()))


HOLD = pltpu.VMEM
LIMIT = 56 << 20
TAIL_LIMIT = 16 << 20


def mm(a, b, dims):
    return lax.dot_general(a, b, dims, preferred_element_type=F32)


def chunk_of(size):
    for width in (512, 384, 256, 128):
        if size % width == 0:
            return width
    return size


def kernel(
    n_e, n_p, n_d,
    tok_hbm, phi_ref, win_hbm, wout_hbm, so_hbm, go_hbm,
    low, sp, phit_ref, gw1, gw2,
    tok3, go3, tok, go, so, win, wout, disp, comb, zg, recv, act, dpre,
    back, bin_, ret, sigr, phi_acc, ps, pr, qb, fin,
    in_sem, w_sem,
    a_send, a_recv, y_send, y_recv, c_send, c_recv, c2_send, c2_recv,
    b_send, b_recv, r_send, r_recv, p_send, p_recv, q_send, q_recv, f_send, f_recv, own_sem,
):
    e = lax.axis_index("expert")
    p = lax.axis_index("pair")
    d = lax.axis_index("dp")
    toks, images, width = tok3.shape
    slots_all = phit_ref.shape[0]
    rows = zg.shape[2]
    slots = rows // images
    hidden = win.shape[1]
    fc = chunk_of(hidden)
    half = width // n_d
    n_lo, n_hi = fin.shape[0], qb.shape[0]
    e_hi, e_lo = e // n_lo, e % n_lo

    def dev(ee, pp, dd):
        return {"expert": ee, "pair": pp, "dp": dd}

    def rem(x, n):
        return lax.rem(x, n)

    def rcopy(src, dst, ss, rs, where):
        return pltpu.make_async_remote_copy(
            src_ref=src, dst_ref=dst, send_sem=ss, recv_sem=rs, device_id=where, device_id_type=MESH
        )

    e_at = [rem(e + k, n_e) for k in range(n_e)]
    e_from = [rem(e + n_e - k, n_e) for k in range(n_e)]
    p_at = [rem(p + k, n_p) for k in range(n_p)]
    p_from = [rem(p + n_p - k, n_p) for k in range(n_p)]
    d_at = [rem(d + k, n_d) for k in range(n_d)]
    d_from = [rem(d + n_d - k, n_d) for k in range(n_d)]

    barrier = pltpu.get_barrier_semaphore()
    peers = [dev(e_at[k], p, d) for k in range(1, n_e)]
    peers += [dev(e, p_at[i], d_at[j]) for i in range(n_p) for j in range(n_d) if i or j]
    lo_at = [e_hi * n_lo + rem(e_lo + k, n_lo) for k in range(n_lo)]
    plane = [(a, i, j) for a in range(n_lo) for i in range(n_p) for j in range(n_d) if a or i or j]
    peers += [dev(lo_at[a], p_at[i], d_at[j]) for a, i, j in plane if a and (i or j)]
    for peer in peers:
        pl.semaphore_signal(barrier, inc=1, device_id=peer, device_id_type=MESH)

    loads = [
        pltpu.make_async_copy(tok_hbm, tok3, in_sem.at[0]),
        pltpu.make_async_copy(go_hbm, go3, in_sem.at[1]),
    ]
    for load in loads:
        load.start()
    w_loads = [
        pltpu.make_async_copy(win_hbm.at[0], win, w_sem.at[0]),
        pltpu.make_async_copy(wout_hbm.at[0], wout, w_sem.at[1]),
        pltpu.make_async_copy(so_hbm, so, w_sem.at[2]),
    ]
    for w_load in w_loads:
        w_load.start()

    total = images * slots_all
    lanes = toks * images

    def pick(columns, index_of):
        r_at = lax.broadcasted_iota(jnp.int32, (total, columns), 0)
        c_at = lax.broadcasted_iota(jnp.int32, (total, columns), 1)
        return jnp.where(index_of(r_at) == c_at, 1.0, 0.0).astype(BF16)

    def slot_of(r):
        return (r // rows) * slots + r % slots

    def image_of(r):
        return (r % rows) // slots

    phi_x = mm(pick(slots_all, slot_of), phi_ref[...], NN).astype(BF16)
    sp[pl.ds(total, total), :] = phi_x
    r_at = lax.broadcasted_iota(jnp.int32, (total, lanes), 0)
    l_at = lax.broadcasted_iota(jnp.int32, (total, lanes), 1)
    same = image_of(r_at) == l_at % images

    loads[0].wait()
    tok[...] = tok3[...].reshape(lanes, width)
    logits = jnp.where(same, mm(phi_x, tok[...], NT), -jnp.inf)
    by_tok = jnp.exp(logits - jnp.max(logits, axis=1, keepdims=True))
    by_tok = by_tok / jnp.sum(by_tok, axis=1, keepdims=True)
    disp[...] = by_tok
    low[pl.ds(0, total), :] = by_tok.astype(BF16)
    zg[0] = mm(by_tok.astype(BF16), tok[...], NN).astype(BF16).reshape(n_e, rows, width)
    by_slot = jnp.exp(logits - jnp.max(logits, axis=0, keepdims=True))
    by_slot = by_slot / jnp.sum(by_slot, axis=0, keepdims=True)
    comb[...] = by_slot
    loads[1].wait()
    go[...] = go3[...].reshape(lanes, width)
    zg[1] = mm(by_slot.astype(BF16), go[...], NN).astype(BF16).reshape(n_e, rows, width)

    pl.semaphore_wait(barrier, len(peers))

    out_a = []
    for k in range(1, n_e):
        cp = rcopy(
            zg.at[:, e_at[k]], recv.at[:, d, p, e], a_send.at[k], a_recv.at[k], dev(e_at[k], p, d)
        )
        cp.start()
        out_a.append(cp)
    own = pltpu.make_async_copy(zg.at[:, e], recv.at[:, d, p, e], own_sem.at[0])
    own.start()

    w_loads[2].wait()
    so_x = mm(
        pick(total, lambda r: image_of(r) * slots_all + slot_of(r)), so[...].reshape(total, width), NN
    ).astype(BF16)
    cm = comb[...]
    cg = mm(so_x, go[...], NT)
    comb[...] = cm * (cg - jnp.sum(cm * cg, axis=0, keepdims=True))

    out_y, out_c, out_c2 = [], [], []
    for k in range(n_e):
        blk = recv.at[:, d, p, e_from[k]]
        if k == 0:
            own.wait()
        else:
            rcopy(blk, blk, a_send.at[k], a_recv.at[k], dev(e, p, d)).wait_recv()
        for i in range(1, n_p):
            cp = rcopy(blk, blk, c_send.at[i, k], c_recv.at[i, k], dev(e, p_at[i], d))
            cp.start()
            out_c.append(cp)
        for j in range(1, n_d):
            cp = rcopy(blk, blk, y_send.at[j, k], y_recv.at[j, k], dev(e, p, d_at[j]))
            cp.start()
            out_y.append(cp)
    for cp in w_loads[:2]:
        cp.wait()
    for i in range(1, n_p):
        for k in range(n_e):
            blk = recv.at[:, d, p_from[i], e_from[k]]
            rcopy(blk, blk, c_send.at[i, k], c_recv.at[i, k], dev(e, p, d)).wait_recv()

    group_rows = n_p * n_e * rows
    part_rows = n_e * rows
    c1 = math.sqrt(2.0 / math.pi)

    def hidden_pass(group, with_back):
        z = recv[0, group].reshape(group_rows, width)
        g = recv[1, group].reshape(group_rows, width)

        def step(c, carry):
            cols = pl.ds(pl.multiple_of(c * fc, fc), fc)
            x = mm(z, win[:, cols], NN)
            da = mm(g, wout[cols, :], NT)
            x2 = x * x
            th = jnp.tanh(c1 * (x + 0.044715 * (x2 * x)))
            cdf = 0.5 * (1.0 + th)
            slope = cdf + (0.5 * c1) * x * (1.0 - th * th) * (1.0 + (3.0 * 0.044715) * x2)
            act[group, :, cols] = (x * cdf).astype(BF16)
            dp_low = (da * slope).astype(BF16)
            dpre[group, :, cols] = dp_low
            if with_back:
                term = mm(dp_low, win[:, cols], NT).reshape(n_p, part_rows, width)

                @pl.when(c == 0)
                def _():
                    back[...] = term

                @pl.when(c > 0)
                def _():
                    back[...] = back[...] + term

            return carry

        lax.fori_loop(0, hidden // fc, step, 0)

    hidden_pass(d, True)

    out_b = []
    for i in range(1, n_p):
        cp = rcopy(back.at[p_at[i]], bin_.at[i - 1], b_send.at[i], b_recv.at[i], dev(e, p_at[i], d))
        cp.start()
        out_b.append(cp)

    for j in range(1, n_d):
        for k in range(n_e):
            blk = recv.at[:, d_from[j], p, e_from[k]]
            rcopy(blk, blk, y_send.at[j, k], y_recv.at[j, k], dev(e, p, d)).wait_recv()
            for i in range(1, n_p):
                cp = rcopy(blk, blk, c2_send.at[j, i, k], c2_recv.at[j, i, k], dev(e, p_at[i], d))
                cp.start()
                out_c2.append(cp)

    acc = back[p]
    for i in range(1, n_p):
        rcopy(bin_.at[i - 1], bin_.at[i - 1], b_send.at[i], b_recv.at[i], dev(e, p, d)).wait_recv()
        acc = acc + bin_[i - 1]
    ret[...] = acc.astype(BF16).reshape(n_e, rows, width)
    out_r = []
    for k in range(1, n_e):
        cp = rcopy(ret.at[e_at[k]], sigr.at[e], r_send.at[k], r_recv.at[k], dev(e_at[k], p, d))
        cp.start()
        out_r.append(cp)
    sigr[e] = ret[e]

    for j in range(1, n_d):
        for i in range(1, n_p):
            for k in range(n_e):
                blk = recv.at[:, d_from[j], p_from[i], e_from[k]]
                rcopy(blk, blk, c2_send.at[j, i, k], c2_recv.at[j, i, k], dev(e, p, d)).wait_recv()
        hidden_pass(d_from[j], False)

    my_half = pl.ds(pl.multiple_of(d * half, half), half)

    def grads_in(c, carry):
        cols = pl.ds(pl.multiple_of(c * fc, fc), fc)
        s1 = None
        for gi in range(n_d):
            z = recv[0, gi, :, :, :, my_half].reshape(group_rows, half)
            g1 = mm(z, dpre[gi, :, cols], TN).astype(BF16).astype(F32)
            s1 = g1 if s1 is None else s1 + g1
        gw1[:, cols] = s1.astype(BF16)
        return carry

    def grads_out(c, carry):
        cols = pl.ds(pl.multiple_of(c * fc, fc), fc)
        s2 = None
        for gi in range(n_d):
            g = recv[1, gi, :, :, :, my_half].reshape(group_rows, half)
            g2 = mm(act[gi, :, cols], g, TN).astype(BF16).astype(F32)
            s2 = g2 if s2 is None else s2 + g2
        gw2[cols, :] = s2.astype(BF16)
        return carry

    lax.fori_loop(0, hidden // fc, grads_in, 0)

    for k in range(1, n_e):
        blk = sigr.at[e_from[k]]
        rcopy(blk, blk, r_send.at[k], r_recv.at[k], dev(e, p, d)).wait_recv()

    sig = sigr[...].reshape(total, width)
    dg = mm(sig, tok[...], NT)
    dm = disp[...]
    lg_low = (dm * (dg - jnp.sum(dm * dg, axis=1, keepdims=True)) + comb[...]).astype(BF16)
    phi_acc[...] = mm(lg_low, tok[...], NN)
    per = ps.shape[3]
    for k in range(n_e):
        piece = None
        for b in range(images):
            term = phi_acc[pl.ds(k * rows + b * slots, slots), :]
            piece = term if piece is None else piece + term
        at, off = (k * slots) // per, (k * slots) % per
        ps[at // (n_p * n_d), (at // n_d) % n_p, at % n_d, pl.ds(off, slots), :] = piece

    def lo_from(k):
        return rem(e_lo + n_lo - k, n_lo)

    out_p = []
    for a, i, j in plane:
        cp = rcopy(
            ps.at[rem(e_lo + a, n_lo), p_at[i], d_at[j]], pr.at[e_lo, p, d],
            p_send.at[a, i, j], p_recv.at[a, i, j], dev(lo_at[a], p_at[i], d_at[j]),
        )
        cp.start()
        out_p.append(cp)
    pr[e_lo, p, d] = ps[e_lo, p, d]

    low[pl.ds(total, total), :] = lg_low
    sp[pl.ds(0, total), :] = sig
    lax.fori_loop(0, hidden // fc, grads_out, 0)

    for a, i, j in plane:
        blk = pr.at[lo_from(a), p_from[i], d_from[j]]
        rcopy(blk, blk, p_send.at[a, i, j], p_recv.at[a, i, j], dev(e, p, d)).wait_recv()
    qb[e_hi] = jnp.sum(pr[...], axis=(0, 1, 2))
    out_q = []
    for k in range(1, n_hi):
        to = rem(e + k * n_lo, n_e)
        cp = rcopy(qb.at[e_hi], qb.at[e_hi], q_send.at[k], q_recv.at[k], dev(to, p, d))
        cp.start()
        out_q.append(cp)
    for group in (out_a, out_y, out_c, out_c2, out_b, out_r, out_p):
        for cp in group:
            cp.wait_send()
    for k in range(1, n_hi):
        blk = qb.at[rem(e_hi + n_hi - k, n_hi)]
        rcopy(blk, blk, q_send.at[k], q_recv.at[k], dev(e, p, d)).wait_recv()
    fin[e_lo, p, d] = jnp.sum(qb[...], axis=0)
    out_f = []
    for a, i, j in plane:
        mine = fin.at[e_lo, p, d]
        cp = rcopy(mine, mine, f_send.at[a, i, j], f_recv.at[a, i, j], dev(lo_at[a], p_at[i], d_at[j]))
        cp.start()
        out_f.append(cp)
    for cp in out_q:
        cp.wait_send()
    for a, i, j in plane:
        blk = fin.at[lo_from(a), p_from[i], d_from[j]]
        rcopy(blk, blk, f_send.at[a, i, j], f_recv.at[a, i, j], dev(e, p, d)).wait_recv()
    for at in range(n_lo * n_p * n_d):
        phit_ref[pl.ds(at * per, per), :] = fin[at // (n_p * n_d), (at // n_d) % n_p, at % n_d]
    for cp in out_f:
        cp.wait_send()


def finish(low, sp, phi_ref, gw1, gw2, tg_hbm, phi_out, gw1_hbm, gw2_hbm, tg, sem):
    toks, images, width = tg.shape
    outs = [
        pltpu.make_async_copy(gw1, gw1_hbm.at[0], sem.at[0]),
        pltpu.make_async_copy(gw2, gw2_hbm.at[0], sem.at[1]),
    ]
    for cp in outs:
        cp.start()
    phi_out[...] = phi_ref[...]
    low_t = low[...].T
    part = width // 2 if width % 256 == 0 else width
    for c in range(width // part):
        cols = pl.ds(c * part, part)
        tg[:, :, cols] = mm(low_t, sp[:, cols], NN).astype(BF16).reshape(toks, images, part)
        cp = pltpu.make_async_copy(tg.at[:, :, cols], tg_hbm.at[:, :, cols], sem.at[2 + c])
        cp.start()
        outs.append(cp)
    for cp in outs:
        cp.wait()


def local(n_e, n_p, n_d, tokens, phi, w_in, w_out, slot_out, grad_out):
    images, toks, width = tokens.shape
    slots_all = phi.shape[1]
    hidden = w_in.shape[2]
    slots = slots_all // n_e
    rows = images * slots
    half = width // n_d
    group = n_p * n_e * rows
    n_lo = 2 if n_e % 2 == 0 else 1
    per = slots_all // (n_lo * n_p * n_d)
    total = images * slots_all
    vm = pltpu.VMEM
    sem = pltpu.SemaphoreType.DMA
    pieces = (n_lo, n_p, n_d, per, width)
    scratch = [
        vm((toks, images, width), BF16),
        vm((toks, images, width), BF16),
        vm((toks * images, width), BF16),
        vm((toks * images, width), BF16),
        vm((images, slots_all, width), BF16),
        vm((width, hidden), BF16),
        vm((hidden, width), BF16),
        vm((total, toks * images), F32),
        vm((total, toks * images), F32),
        vm((2, n_e, rows, width), BF16),
        vm((2, n_d, n_p, n_e, rows, width), BF16),
        vm((n_d, group, hidden), BF16),
        vm((n_d, group, hidden), BF16),
        vm((n_p, n_e * rows, width), F32),
        vm((n_p - 1, n_e * rows, width), F32),
        vm((n_e, rows, width), BF16),
        vm((n_e, rows, width), BF16),
        vm((total, width), F32),
        vm(pieces, F32),
        vm(pieces, F32),
        vm((n_e // n_lo, per, width), F32),
        vm(pieces, F32),
        sem((2,)),
        sem((3,)),
    ]
    scratch += [sem((n_e,))] * 2
    scratch += [sem((n_d, n_e))] * 2
    scratch += [sem((n_p, n_e))] * 2
    scratch += [sem((n_d, n_p, n_e))] * 2
    scratch += [sem((n_p,))] * 2
    scratch += [sem((n_e,))] * 2
    scratch += [sem((n_lo, n_p, n_d))] * 2
    scratch += [sem((n_e // n_lo,))] * 2
    scratch += [sem((n_lo, n_p, n_d))] * 2
    scratch += [sem((1,))]
    hbm = pl.BlockSpec(memory_space=pl.ANY)
    vmem = pl.BlockSpec(memory_space=pltpu.VMEM)
    struct = jax.ShapeDtypeStruct
    passed = pl.pallas_call(
        functools.partial(kernel, n_e, n_p, n_d),
        out_shape=tuple(
            HOLD(shape, dtype)
            for shape, dtype in (
                ((2 * total, toks * images), BF16),
                ((2 * total, width), BF16),
                ((slots_all, width), F32),
                ((half, hidden), BF16),
                ((hidden, half), BF16),
            )
        ),
        in_specs=[hbm, vmem, hbm, hbm, hbm, hbm],
        out_specs=(vmem,) * 5,
        scratch_shapes=scratch,
        compiler_params=pltpu.CompilerParams(collective_id=0, has_side_effects=True, vmem_limit_bytes=LIMIT),
    )(jnp.transpose(tokens, (1, 0, 2)), phi.T, w_in, w_out, slot_out, jnp.transpose(grad_out, (1, 0, 2)))
    token_grad, phi_t, gw1, gw2 = pl.pallas_call(
        finish,
        out_shape=(
            struct((toks, images, width), BF16),
            struct((slots_all, width), F32),
            struct((1, half, hidden), BF16),
            struct((1, hidden, half), BF16),
        ),
        in_specs=[vmem] * 5,
        out_specs=(hbm, vmem, hbm, hbm),
        scratch_shapes=[vm((toks, images, width), BF16), sem((4,))],
        compiler_params=pltpu.CompilerParams(vmem_limit_bytes=TAIL_LIMIT),
    )(*(pltpu.with_memory_space_constraint(x, pltpu.VMEM) for x in passed))
    return (jnp.transpose(token_grad, (1, 0, 2)), phi_t.T, gw1, gw2)


def solution(mesh):
    in_specs = (
        P(("expert", "pair", "dp"), None, None),
        P(),
        P("expert", None, "pair"),
        P("expert", "pair", None),
        P(("expert", "pair", "dp"), None, None),
        P(("expert", "pair", "dp"), None, None),
    )
    out_specs = (
        P(("expert", "pair", "dp"), None, None),
        P(),
        P("expert", "dp", "pair"),
        P("expert", "pair", "dp"),
    )
    body = functools.partial(local, mesh.shape["expert"], mesh.shape["pair"], mesh.shape["dp"])
    return jax.shard_map(body, mesh=mesh, in_specs=in_specs, out_specs=out_specs, check_vma=False)
```

```python
import functools
import math

import jax
import jax.numpy as jnp
from jax import lax
from jax.experimental import pallas as pl
from jax.experimental.pallas import tpu as pltpu
from jax.sharding import PartitionSpec as P

MESH = pl.DeviceIdType.MESH
F32 = jnp.float32
BF16 = jnp.bfloat16
NN = (((1,), (0,)), ((), ()))
NT = (((1,), (1,)), ((), ()))
TN = (((0,), (0,)), ((), ()))


HOLD = pltpu.VMEM
LIMIT = 56 << 20
TAIL_LIMIT = 16 << 20


def mm(a, b, dims):
    return lax.dot_general(a, b, dims, preferred_element_type=F32)


def chunk_of(size):
    for width in (512, 384, 256, 128):
        if size % width == 0:
            return width
    return size


def kernel(
    n_e, n_p, n_d,
    tok_hbm, phi_ref, win_hbm, wout_hbm, so_hbm, go_hbm,
    tg, phit_ref, gw1, gw2,
    low, sp, tok3, go3, tok, go, so, win, wout, disp, comb, zg, recv, act, dpre,
    back, bin_, ret, sigr, phi_acc, ps, pr, qb, fin,
    in_sem, w_sem,
    a_send, a_recv, y_send, y_recv, c_send, c_recv, c2_send, c2_recv,
    b_send, b_recv, r_send, r_recv, p_send, p_recv, q_send, q_recv, f_send, f_recv, own_sem,
):
    e = lax.axis_index("expert")
    p = lax.axis_index("pair")
    d = lax.axis_index("dp")
    toks, images, width = tok3.shape
    slots_all = phit_ref.shape[0]
    rows = zg.shape[2]
    slots = rows // images
    hidden = win.shape[1]
    fc = chunk_of(hidden)
    half = width // n_d
    n_lo, n_hi = fin.shape[0], qb.shape[0]
    e_hi, e_lo = e // n_lo, e % n_lo

    def dev(ee, pp, dd):
        return {"expert": ee, "pair": pp, "dp": dd}

    def rem(x, n):
        return lax.rem(x, n)

    def rcopy(src, dst, ss, rs, where):
        return pltpu.make_async_remote_copy(
            src_ref=src, dst_ref=dst, send_sem=ss, recv_sem=rs, device_id=where, device_id_type=MESH
        )

    e_at = [rem(e + k, n_e) for k in range(n_e)]
    e_from = [rem(e + n_e - k, n_e) for k in range(n_e)]
    p_at = [rem(p + k, n_p) for k in range(n_p)]
    p_from = [rem(p + n_p - k, n_p) for k in range(n_p)]
    d_at = [rem(d + k, n_d) for k in range(n_d)]
    d_from = [rem(d + n_d - k, n_d) for k in range(n_d)]

    barrier = pltpu.get_barrier_semaphore()
    peers = [dev(e_at[k], p, d) for k in range(1, n_e)]
    peers += [dev(e, p_at[i], d_at[j]) for i in range(n_p) for j in range(n_d) if i or j]
    lo_at = [e_hi * n_lo + rem(e_lo + k, n_lo) for k in range(n_lo)]
    plane = [(a, i, j) for a in range(n_lo) for i in range(n_p) for j in range(n_d) if a or i or j]
    peers += [dev(lo_at[a], p_at[i], d_at[j]) for a, i, j in plane if a and (i or j)]
    for peer in peers:
        pl.semaphore_signal(barrier, inc=1, device_id=peer, device_id_type=MESH)

    loads = [
        pltpu.make_async_copy(tok_hbm, tok3, in_sem.at[0]),
        pltpu.make_async_copy(go_hbm, go3, in_sem.at[1]),
    ]
    for load in loads:
        load.start()
    w_loads = [
        pltpu.make_async_copy(win_hbm.at[0], win, w_sem.at[0]),
        pltpu.make_async_copy(wout_hbm.at[0], wout, w_sem.at[1]),
        pltpu.make_async_copy(so_hbm, so, w_sem.at[2]),
    ]
    for w_load in w_loads:
        w_load.start()

    total = images * slots_all
    lanes = toks * images

    def pick(columns, index_of):
        r_at = lax.broadcasted_iota(jnp.int32, (total, columns), 0)
        c_at = lax.broadcasted_iota(jnp.int32, (total, columns), 1)
        return jnp.where(index_of(r_at) == c_at, 1.0, 0.0).astype(BF16)

    def slot_of(r):
        return (r // rows) * slots + r % slots

    def image_of(r):
        return (r % rows) // slots

    phi_x = mm(pick(slots_all, slot_of), phi_ref[...], NN).astype(BF16)
    sp[pl.ds(total, total), :] = phi_x
    r_at = lax.broadcasted_iota(jnp.int32, (total, lanes), 0)
    l_at = lax.broadcasted_iota(jnp.int32, (total, lanes), 1)
    same = image_of(r_at) == l_at % images

    loads[0].wait()
    tok[...] = tok3[...].reshape(lanes, width)
    logits = jnp.where(same, mm(phi_x, tok[...], NT), -jnp.inf)
    by_tok = jnp.exp(logits - jnp.max(logits, axis=1, keepdims=True))
    by_tok = by_tok / jnp.sum(by_tok, axis=1, keepdims=True)
    disp[...] = by_tok
    low[pl.ds(0, total), :] = by_tok.astype(BF16)
    zg[0] = mm(by_tok.astype(BF16), tok[...], NN).astype(BF16).reshape(n_e, rows, width)
    pl.semaphore_wait(barrier, len(peers))

    out_a = []
    for k in range(1, n_e):
        cp = rcopy(
            zg.at[0, e_at[k]], recv.at[0, d, p, e],
            a_send.at[0, k], a_recv.at[0, k], dev(e_at[k], p, d),
        )
        cp.start()
        out_a.append(cp)
    by_slot = jnp.exp(logits - jnp.max(logits, axis=0, keepdims=True))
    by_slot = by_slot / jnp.sum(by_slot, axis=0, keepdims=True)
    comb[...] = by_slot
    loads[1].wait()
    go[...] = go3[...].reshape(lanes, width)
    zg[1] = mm(by_slot.astype(BF16), go[...], NN).astype(BF16).reshape(n_e, rows, width)

    for k in range(1, n_e):
        cp = rcopy(
            zg.at[1, e_at[k]], recv.at[1, d, p, e],
            a_send.at[1, k], a_recv.at[1, k], dev(e_at[k], p, d),
        )
        cp.start()
        out_a.append(cp)
    own = pltpu.make_async_copy(zg.at[:, e], recv.at[:, d, p, e], own_sem.at[0])
    own.start()

    w_loads[2].wait()
    so_x = mm(
        pick(total, lambda r: image_of(r) * slots_all + slot_of(r)), so[...].reshape(total, width), NN
    ).astype(BF16)
    cm = comb[...]
    cg = mm(so_x, go[...], NT)
    comb[...] = cm * (cg - jnp.sum(cm * cg, axis=0, keepdims=True))

    out_y, out_c, out_c2 = [], [], []
    for k in range(n_e):
        blk = recv.at[:, d, p, e_from[k]]
        if k == 0:
            own.wait()
        else:
            for w in range(2):
                half_blk = recv.at[w, d, p, e_from[k]]
                rcopy(half_blk, half_blk, a_send.at[w, k], a_recv.at[w, k], dev(e, p, d)).wait_recv()
        for i in range(1, n_p):
            cp = rcopy(blk, blk, c_send.at[i, k], c_recv.at[i, k], dev(e, p_at[i], d))
            cp.start()
            out_c.append(cp)
        for j in range(1, n_d):
            cp = rcopy(blk, blk, y_send.at[j, k], y_recv.at[j, k], dev(e, p, d_at[j]))
            cp.start()
            out_y.append(cp)
    for cp in w_loads[:2]:
        cp.wait()
    for i in range(1, n_p):
        for k in range(n_e):
            blk = recv.at[:, d, p_from[i], e_from[k]]
            rcopy(blk, blk, c_send.at[i, k], c_recv.at[i, k], dev(e, p, d)).wait_recv()

    group_rows = n_p * n_e * rows
    part_rows = n_e * rows
    c1 = math.sqrt(2.0 / math.pi)

    def hidden_pass(group, with_back):
        z = recv[0, group].reshape(group_rows, width)
        g = recv[1, group].reshape(group_rows, width)

        def step(c, carry):
            cols = pl.ds(pl.multiple_of(c * fc, fc), fc)
            x = mm(z, win[:, cols], NN)
            da = mm(g, wout[cols, :], NT)
            x2 = x * x
            th = jnp.tanh(c1 * (x + 0.044715 * (x2 * x)))
            cdf = 0.5 * (1.0 + th)
            slope = cdf + (0.5 * c1) * x * (1.0 - th * th) * (1.0 + (3.0 * 0.044715) * x2)
            act[group, :, cols] = (x * cdf).astype(BF16)
            dp_low = (da * slope).astype(BF16)
            dpre[group, :, cols] = dp_low
            if with_back:
                term = mm(dp_low, win[:, cols], NT).reshape(n_p, part_rows, width)

                @pl.when(c == 0)
                def _():
                    back[...] = term

                @pl.when(c > 0)
                def _():
                    back[...] = back[...] + term

            return carry

        lax.fori_loop(0, hidden // fc, step, 0)

    hidden_pass(d, True)

    out_b = []
    for i in range(1, n_p):
        cp = rcopy(back.at[p_at[i]], bin_.at[i - 1], b_send.at[i], b_recv.at[i], dev(e, p_at[i], d))
        cp.start()
        out_b.append(cp)

    acc = back[p]
    for i in range(1, n_p):
        rcopy(bin_.at[i - 1], bin_.at[i - 1], b_send.at[i], b_recv.at[i], dev(e, p, d)).wait_recv()
        acc = acc + bin_[i - 1]
    ret[...] = acc.astype(BF16).reshape(n_e, rows, width)
    out_r = []
    for k in range(1, n_e):
        cp = rcopy(ret.at[e_at[k]], sigr.at[e], r_send.at[k], r_recv.at[k], dev(e_at[k], p, d))
        cp.start()
        out_r.append(cp)
    sigr[e] = ret[e]

    for j in range(1, n_d):
        for k in range(n_e):
            blk = recv.at[:, d_from[j], p, e_from[k]]
            rcopy(blk, blk, y_send.at[j, k], y_recv.at[j, k], dev(e, p, d)).wait_recv()
            for i in range(1, n_p):
                cp = rcopy(blk, blk, c2_send.at[j, i, k], c2_recv.at[j, i, k], dev(e, p_at[i], d))
                cp.start()
                out_c2.append(cp)

    for j in range(1, n_d):
        for i in range(1, n_p):
            for k in range(n_e):
                blk = recv.at[:, d_from[j], p_from[i], e_from[k]]
                rcopy(blk, blk, c2_send.at[j, i, k], c2_recv.at[j, i, k], dev(e, p, d)).wait_recv()
        hidden_pass(d_from[j], False)

    my_half = pl.ds(pl.multiple_of(d * half, half), half)

    def grads_in(c, carry):
        cols = pl.ds(pl.multiple_of(c * fc, fc), fc)
        s1 = None
        for gi in range(n_d):
            z = recv[0, gi, :, :, :, my_half].reshape(group_rows, half)
            g1 = mm(z, dpre[gi, :, cols], TN).astype(BF16).astype(F32)
            s1 = g1 if s1 is None else s1 + g1
        gw1[:, cols] = s1.astype(BF16)
        return carry

    def grads_out(c, carry):
        cols = pl.ds(pl.multiple_of(c * fc, fc), fc)
        s2 = None
        for gi in range(n_d):
            g = recv[1, gi, :, :, :, my_half].reshape(group_rows, half)
            g2 = mm(act[gi, :, cols], g, TN).astype(BF16).astype(F32)
            s2 = g2 if s2 is None else s2 + g2
        gw2[cols, :] = s2.astype(BF16)
        return carry

    lax.fori_loop(0, hidden // fc, grads_in, 0)

    for k in range(1, n_e):
        blk = sigr.at[e_from[k]]
        rcopy(blk, blk, r_send.at[k], r_recv.at[k], dev(e, p, d)).wait_recv()

    sig = sigr[...].reshape(total, width)
    dg = mm(sig, tok[...], NT)
    dm = disp[...]
    lg_low = (dm * (dg - jnp.sum(dm * dg, axis=1, keepdims=True)) + comb[...]).astype(BF16)
    phi_acc[...] = mm(lg_low, tok[...], NN)
    per = ps.shape[3]
    for k in range(n_e):
        piece = None
        for b in range(images):
            term = phi_acc[pl.ds(k * rows + b * slots, slots), :]
            piece = term if piece is None else piece + term
        at, off = (k * slots) // per, (k * slots) % per
        ps[at // (n_p * n_d), (at // n_d) % n_p, at % n_d, pl.ds(off, slots), :] = piece

    def lo_from(k):
        return rem(e_lo + n_lo - k, n_lo)

    out_p = []
    for a, i, j in plane:
        cp = rcopy(
            ps.at[rem(e_lo + a, n_lo), p_at[i], d_at[j]], pr.at[e_lo, p, d],
            p_send.at[a, i, j], p_recv.at[a, i, j], dev(lo_at[a], p_at[i], d_at[j]),
        )
        cp.start()
        out_p.append(cp)
    pr[e_lo, p, d] = ps[e_lo, p, d]

    low[pl.ds(total, total), :] = lg_low
    sp[pl.ds(0, total), :] = sig
    lax.fori_loop(0, hidden // fc, grads_out, 0)

    for a, i, j in plane:
        blk = pr.at[lo_from(a), p_from[i], d_from[j]]
        rcopy(blk, blk, p_send.at[a, i, j], p_recv.at[a, i, j], dev(e, p, d)).wait_recv()
    qb[e_hi] = jnp.sum(pr[...], axis=(0, 1, 2))
    out_q = []
    for k in range(1, n_hi):
        to = rem(e + k * n_lo, n_e)
        cp = rcopy(qb.at[e_hi], qb.at[e_hi], q_send.at[k], q_recv.at[k], dev(to, p, d))
        cp.start()
        out_q.append(cp)
    for group in (out_a, out_y, out_c, out_c2, out_b, out_r, out_p):
        for cp in group:
            cp.wait_send()
    tg[...] = mm(low[...], sp[...], TN).astype(BF16).reshape(toks, images, width)
    for k in range(1, n_hi):
        blk = qb.at[rem(e_hi + n_hi - k, n_hi)]
        rcopy(blk, blk, q_send.at[k], q_recv.at[k], dev(e, p, d)).wait_recv()
    fin[e_lo, p, d] = jnp.sum(qb[...], axis=0)
    out_f = []
    for a, i, j in plane:
        mine = fin.at[e_lo, p, d]
        cp = rcopy(mine, mine, f_send.at[a, i, j], f_recv.at[a, i, j], dev(lo_at[a], p_at[i], d_at[j]))
        cp.start()
        out_f.append(cp)
    for cp in out_q:
        cp.wait_send()
    for a, i, j in plane:
        blk = fin.at[lo_from(a), p_from[i], d_from[j]]
        rcopy(blk, blk, f_send.at[a, i, j], f_recv.at[a, i, j], dev(e, p, d)).wait_recv()
    for at in range(n_lo * n_p * n_d):
        phit_ref[pl.ds(at * per, per), :] = fin[at // (n_p * n_d), (at // n_d) % n_p, at % n_d]
    for cp in out_f:
        cp.wait_send()


def finish(tg, phi_ref, gw1, gw2, tg_hbm, phi_out, gw1_hbm, gw2_hbm, sem):
    cut = tg.shape[0] // 2
    outs = [
        pltpu.make_async_copy(tg.at[:cut], tg_hbm.at[:cut], sem.at[0]),
        pltpu.make_async_copy(tg.at[cut:], tg_hbm.at[cut:], sem.at[1]),
        pltpu.make_async_copy(gw1, gw1_hbm.at[0], sem.at[2]),
        pltpu.make_async_copy(gw2, gw2_hbm.at[0], sem.at[3]),
    ]
    for cp in outs:
        cp.start()
    phi_out[...] = phi_ref[...]
    for cp in outs:
        cp.wait()


def local(n_e, n_p, n_d, tokens, phi, w_in, w_out, slot_out, grad_out):
    images, toks, width = tokens.shape
    slots_all = phi.shape[1]
    hidden = w_in.shape[2]
    slots = slots_all // n_e
    rows = images * slots
    half = width // n_d
    group = n_p * n_e * rows
    n_lo = 2 if n_e % 2 == 0 else 1
    per = slots_all // (n_lo * n_p * n_d)
    total = images * slots_all
    vm = pltpu.VMEM
    sem = pltpu.SemaphoreType.DMA
    pieces = (n_lo, n_p, n_d, per, width)
    scratch = [
        vm((2 * total, toks * images), BF16),
        vm((2 * total, width), BF16),
        vm((toks, images, width), BF16),
        vm((toks, images, width), BF16),
        vm((toks * images, width), BF16),
        vm((toks * images, width), BF16),
        vm((images, slots_all, width), BF16),
        vm((width, hidden), BF16),
        vm((hidden, width), BF16),
        vm((total, toks * images), F32),
        vm((total, toks * images), F32),
        vm((2, n_e, rows, width), BF16),
        vm((2, n_d, n_p, n_e, rows, width), BF16),
        vm((n_d, group, hidden), BF16),
        vm((n_d, group, hidden), BF16),
        vm((n_p, n_e * rows, width), F32),
        vm((n_p - 1, n_e * rows, width), F32),
        vm((n_e, rows, width), BF16),
        vm((n_e, rows, width), BF16),
        vm((total, width), F32),
        vm(pieces, F32),
        vm(pieces, F32),
        vm((n_e // n_lo, per, width), F32),
        vm(pieces, F32),
        sem((2,)),
        sem((3,)),
    ]
    scratch += [sem((2, n_e))] * 2
    scratch += [sem((n_d, n_e))] * 2
    scratch += [sem((n_p, n_e))] * 2
    scratch += [sem((n_d, n_p, n_e))] * 2
    scratch += [sem((n_p,))] * 2
    scratch += [sem((n_e,))] * 2
    scratch += [sem((n_lo, n_p, n_d))] * 2
    scratch += [sem((n_e // n_lo,))] * 2
    scratch += [sem((n_lo, n_p, n_d))] * 2
    scratch += [sem((1,))]
    hbm = pl.BlockSpec(memory_space=pl.ANY)
    vmem = pl.BlockSpec(memory_space=pltpu.VMEM)
    struct = jax.ShapeDtypeStruct
    passed = pl.pallas_call(
        functools.partial(kernel, n_e, n_p, n_d),
        out_shape=tuple(
            HOLD(shape, dtype)
            for shape, dtype in (
                ((toks, images, width), BF16),
                ((slots_all, width), F32),
                ((half, hidden), BF16),
                ((hidden, half), BF16),
            )
        ),
        in_specs=[hbm, vmem, hbm, hbm, hbm, hbm],
        out_specs=(vmem,) * 4,
        scratch_shapes=scratch,
        compiler_params=pltpu.CompilerParams(collective_id=0, has_side_effects=True, vmem_limit_bytes=LIMIT),
    )(jnp.transpose(tokens, (1, 0, 2)), phi.T, w_in, w_out, slot_out, jnp.transpose(grad_out, (1, 0, 2)))
    token_grad, phi_t, gw1, gw2 = pl.pallas_call(
        finish,
        out_shape=(
            struct((toks, images, width), BF16),
            struct((slots_all, width), F32),
            struct((1, half, hidden), BF16),
            struct((1, hidden, half), BF16),
        ),
        in_specs=[vmem] * 4,
        out_specs=(hbm, vmem, hbm, hbm),
        scratch_shapes=[sem((4,))],
        compiler_params=pltpu.CompilerParams(vmem_limit_bytes=TAIL_LIMIT),
    )(*(pltpu.with_memory_space_constraint(x, pltpu.VMEM) for x in passed))
    return (jnp.transpose(token_grad, (1, 0, 2)), phi_t.T, gw1, gw2)


def solution(mesh):
    in_specs = (
        P(("expert", "pair", "dp"), None, None),
        P(),
        P("expert", None, "pair"),
        P("expert", "pair", None),
        P(("expert", "pair", "dp"), None, None),
        P(("expert", "pair", "dp"), None, None),
    )
    out_specs = (
        P(("expert", "pair", "dp"), None, None),
        P(),
        P("expert", "dp", "pair"),
        P("expert", "pair", "dp"),
    )
    body = functools.partial(local, mesh.shape["expert"], mesh.shape["pair"], mesh.shape["dp"])
    return jax.shard_map(body, mesh=mesh, in_specs=in_specs, out_specs=out_specs, check_vma=False)
```
